32 devices in a mesh: section: 2 (over y), dp: 16 (over z, x, core).
Axes of the slice: x: 2, y: 2, z: 4, core: 2. Of those that a mesh axis runs over, the one named last changes fastest.
Arguments:
- inputs: bfloat16 [4096, 768], P('dp'), may hold values from -6 to 6
- cotangent: bfloat16 [4096, 768], P('dp'), may hold values from -6 to 6
- segments: int32 [4096], P('dp'), may hold values from 0 to 3, as said below
- qkv_weight: bfloat16 [2, 768, 2304], P('section', 'dp'), may hold values from -0.21875 to 0.21875
- out_weight: bfloat16 [2, 768, 768], P('section', 'dp'), may hold values from -0.875 to 0.875
- up_weight: bfloat16 [2, 768, 3072], P('section', 'dp'), may hold values from -0.21875 to 0.21875
- down_weight: bfloat16 [2, 3072, 768], P('section', 'dp'), may hold values from -0.109375 to 0.109375
- norm_params: bfloat16 [2, 4, 768], P('section', None, 'dp'), may hold values from 0.5 to 1.5
- bias_params: bfloat16 [2, 4, 768], P('section', None, 'dp'), may hold values from -3 to 3
- up_bias: bfloat16 [2, 3072], P('section', 'dp'), may hold values from -3 to 3
Outputs:
- layer_outputs: bfloat16 [2, 4096, 768], P('section', 'dp')
- input_grads: bfloat16 [2, 4096, 768], P('section', 'dp')
- qkv_grad: float32 [2, 768, 2304], P('section', 'dp')
- out_grad: float32 [2, 768, 768], P('section', 'dp')
- up_grad: float32 [2, 768, 3072], P('section', 'dp')
- down_grad: float32 [2, 3072, 768], P('section', 'dp')
- norm_grad: float32 [2, 4, 768], P('section', None, 'dp')
- bias_grad: float32 [2, 4, 768], P('section', None, 'dp')
- up_bias_grad: float32 [2, 3072], P('section', 'dp')
The draws below stay inside these ranges and needn't reach their ends.
Inputs may be any that keep to these rules, and one draw needn't show every extreme that they name: `segments`: within each aligned block of 128 positions the numbers start at 0 and rise by one where a new sequence starts; every block holds exactly 4 sequences; no sequence crosses a block.
All inputs are finite; a program needn't handle non-finite values.
Results may differ from the reference program's by a relative error of at most 0.014.
Values may be sent and summed in bfloat16 or wider, within the bound.
A program may use at most 256 MiB of HBM per device.

```python
import math
import jax
import jax.numpy as jnp
from jax import lax

D = 768
FF = 3072
HEAD = 64
ROT = 16
SEQS = 4
PACK = 128
TOKENS = 4096


def draw_segments(key, part):
    packs = TOKENS // PACK
    key_rows = jax.random.split(key, packs)
    chosen = jax.vmap(lambda one: jax.random.permutation(one, PACK - 1)[:SEQS - 1] + 1)(key_rows)
    index = jnp.arange(PACK, dtype=jnp.int32)
    starts = jnp.any(index[None, None, :] == chosen[:, :, None], axis=1)
    ids = jnp.cumsum(starts.astype(jnp.int32), axis=1)
    return ids.reshape(TOKENS).astype(jnp.int32)


def block_levels(rng, extent, cuts, smallest, high):
    factor_of, own = 1.0, jax.random.fold_in(rng, 6)
    for dim, blocks in cuts:
        draws = jnp.exp(jax.random.uniform(jax.random.fold_in(own, dim), (blocks,), jnp.float32, smallest / len(cuts), high / len(cuts)))
        factor_of = factor_of * jnp.repeat(draws, extent[dim] // blocks).reshape([-1 if axis == dim else 1 for axis in range(len(extent))])
    return factor_of


def noise(stream_key, shape, scale, limit, cuts=(), held_as=jnp.bfloat16):
    values = jax.random.normal(stream_key, shape, jnp.float32) * scale
    if len(cuts) > 0:
        values = block_levels(stream_key, shape, cuts, -0.22, 0.18) * values
    return jnp.clip(values, min=-limit, max=limit).astype(held_as)


def setup_inputs(seed: int = 0) -> dict:
    streams_of = jax.random.split(jax.random.key(seed), 11)
    inputs = noise(streams_of[0], (TOKENS, D), 1.0, 6.0, ((0, 16),))
    cotangent = noise(streams_of[1], (TOKENS, D), 1.0, 6.0, ((0, 16),))
    segments = draw_segments(jax.random.fold_in(streams_of[10], 71), 0)
    qkv_weight = noise(streams_of[3], (2, D, 3 * D), D ** -0.5, 0.21875, ((0, 2), (1, 16)))
    out_weight = noise(streams_of[4], (2, D, D), (D // 16) ** -0.5, 0.875, ((0, 2), (1, 16)))
    up_weight = noise(streams_of[5], (2, D, FF), D ** -0.5, 0.21875, ((0, 2), (1, 16)))
    down_weight = noise(streams_of[6], (2, FF, D), FF ** -0.5, 0.109375, ((0, 2), (1, 16)))
    norm_params = jnp.clip(0.5 + 1.0 * jax.random.uniform(streams_of[7], (2, 4, D), jnp.float32) ** block_levels(streams_of[7], (2, 4, D), ((0, 2), (2, 16)), -0.2, 0.2), 0.5, 1.5).astype(jnp.bfloat16)
    bias_params = noise(streams_of[8], (2, 4, D), 0.5, 3.0, ((0, 2), (2, 16)))
    up_bias = noise(streams_of[9], (2, FF), 0.5, 3.0, ((0, 2), (1, 16)))
    return dict(inputs=inputs, cotangent=cotangent, segments=segments, qkv_weight=qkv_weight, out_weight=out_weight, up_weight=up_weight, down_weight=down_weight, norm_params=norm_params, bias_params=bias_params, up_bias=up_bias)


EPS = 1e-05
HALF_ROOT = 0.7071067811865476
INV_ROOT_TAU = 0.3989422804014327
NEGATIVE = -1e+30

def mix(form, left, right):
    return jnp.einsum(form, left.astype(jnp.float32), right.astype(jnp.float32))

def layer_normalize(input_float, norm_gain, norm_shift):
    row_mean = lax.optimization_barrier(jnp.mean(input_float, axis=-1, keepdims=True))
    centered_input = input_float - row_mean
    inverse_deviation = lax.rsqrt(lax.optimization_barrier(jnp.mean(centered_input * centered_input, axis=-1, keepdims=True)) + EPS)
    standardized_input = centered_input * inverse_deviation
    return (standardized_input, inverse_deviation, (standardized_input * norm_gain + norm_shift).astype(jnp.bfloat16))

def layer_normalize_backward(normed_gradient, standardized_input, inverse_deviation, norm_gain):
    standardized_gradient = normed_gradient * norm_gain
    inner_width = lax.optimization_barrier(jnp.mean(standardized_gradient, axis=-1, keepdims=True)) + standardized_input * lax.optimization_barrier(jnp.mean(standardized_gradient * standardized_input, axis=-1, keepdims=True))
    return (inverse_deviation * (standardized_gradient - inner_width), lax.optimization_barrier(jnp.sum(normed_gradient * standardized_input, axis=0)), lax.optimization_barrier(jnp.sum(normed_gradient, axis=0)))

def rotary_tables(seg):
    width = seg.shape[1]
    index = jnp.broadcast_to(jnp.arange(width, dtype=jnp.int32)[None, :], seg.shape)
    before = jnp.concatenate([seg[:, :1] - 1, seg[:, :-1]], axis=1)
    first = lax.cummax(jnp.where(seg != before, index, 0), axis=1)
    place = (index - first).astype(jnp.float32)
    freq = 10000.0 ** (-jnp.arange(0, ROT, 2, dtype=jnp.float32) / ROT)
    angle = place[:, :, None, None] * freq
    return (jnp.cos(angle), jnp.sin(angle))

def rotate(tensor, cosine, sine, sign):
    half = ROT // 2
    first = tensor[..., :half]
    second = tensor[..., half:ROT]
    return jnp.concatenate([first * cosine - sign * second * sine, second * cosine + sign * first * sine, tensor[..., ROT:]], axis=-1)

def scores(query_rows, key_rows, seg):
    width = seg.shape[1]
    raw = mix('prhe,pshe->phrs', query_rows, key_rows) * (1.0 / math.sqrt(HEAD))
    index = jnp.arange(width, dtype=jnp.int32)
    causal = index[:, None] >= index[None, :]
    allowed = (seg[:, None, :, None] == seg[:, None, None, :]) & causal[None, None]
    return jnp.where(allowed, raw, NEGATIVE)

def forward(x, seg, weights):
    wqkv, wout, wup, wdown, norm_pairs, abias, upbias = weights
    packs, width = seg.shape
    shape = (packs, width, D // HEAD, HEAD)
    norm_pairs = norm_pairs.astype(jnp.float32)
    abias = abias.astype(jnp.float32)
    upbias = upbias.astype(jnp.float32)
    input_float = x.astype(jnp.float32)
    first_standardized, first_inverse_deviation, first_normed = layer_normalize(input_float, norm_pairs[0], norm_pairs[1])
    second_standardized, second_inverse_deviation, second_normed = layer_normalize(input_float, norm_pairs[2], norm_pairs[3])
    qkv = jnp.dot(first_normed, wqkv, preferred_element_type=jnp.float32)
    cosine, sine = rotary_tables(seg)
    query_rows = rotate((qkv[:, :D] + abias[0]).reshape(shape), cosine, sine, 1.0).astype(jnp.bfloat16)
    key_rows = rotate(qkv[:, D:2 * D].reshape(shape), cosine, sine, 1.0).astype(jnp.bfloat16)
    value_rows = (qkv[:, 2 * D:] + abias[1]).reshape(shape).astype(jnp.bfloat16)
    raw = scores(query_rows, key_rows, seg)
    top = lax.optimization_barrier(jnp.max(raw, axis=-1, keepdims=True))
    log_sum_exp = top + jnp.log(lax.optimization_barrier(jnp.sum(jnp.exp(raw - top), axis=-1, keepdims=True)))
    probs = jnp.exp(raw - log_sum_exp).astype(jnp.bfloat16)
    context_rows = mix('phrs,pshe->prhe', probs, value_rows).reshape(packs * width, D).astype(jnp.bfloat16)
    attended = jnp.dot(context_rows, wout, preferred_element_type=jnp.float32) + abias[2]
    hidden_rows = jnp.dot(second_normed, wup, preferred_element_type=jnp.float32) + upbias
    activation_output = (0.5 * hidden_rows * (1.0 + lax.erf(hidden_rows * HALF_ROOT))).astype(jnp.bfloat16)
    mlp = jnp.dot(activation_output, wdown, preferred_element_type=jnp.float32) + abias[3]
    result = (input_float + attended + mlp).astype(jnp.bfloat16)
    saved_state = (first_standardized, first_inverse_deviation, first_normed, second_standardized, second_inverse_deviation, second_normed, query_rows, key_rows, value_rows, log_sum_exp, context_rows, hidden_rows, activation_output)
    return (result, saved_state)

def backward(saved_state, upstream, seg, weights):
    wqkv, wout, wup, wdown, norm_pairs, abias, upbias = weights
    first_standardized, first_inverse_deviation, first_normed, second_standardized, second_inverse_deviation, second_normed, query_rows, key_rows, value_rows, log_sum_exp, context_rows, hidden_rows, activation_output = saved_state
    packs, width = seg.shape
    shape = (packs, width, D // HEAD, HEAD)
    norm_pairs = norm_pairs.astype(jnp.float32)
    upf = upstream.astype(jnp.float32)
    d_down = jnp.dot(activation_output.T, upstream, preferred_element_type=jnp.float32)
    dgelu = jnp.dot(upstream, wdown.T, preferred_element_type=jnp.float32)
    slope = 0.5 * (1.0 + lax.erf(hidden_rows * HALF_ROOT)) + hidden_rows * INV_ROOT_TAU * jnp.exp(-0.5 * hidden_rows * hidden_rows)
    dhidden = dgelu * slope
    dhidden_low = dhidden.astype(jnp.bfloat16)
    d_up = jnp.dot(second_normed.T, dhidden_low, preferred_element_type=jnp.float32)
    second_norm_gradient = jnp.dot(dhidden_low, wup.T, preferred_element_type=jnp.float32)
    d_out = jnp.dot(context_rows.T, upstream, preferred_element_type=jnp.float32)
    dctx = jnp.dot(upstream, wout.T, preferred_element_type=jnp.float32).reshape(shape).astype(jnp.bfloat16)
    probs = jnp.exp(scores(query_rows, key_rows, seg) - log_sum_exp)
    dvalues = mix('phrs,prhe->pshe', probs.astype(jnp.bfloat16), dctx)
    dprobs = mix('prhe,pshe->phrs', dctx, value_rows)
    dscores = (probs * (dprobs - lax.optimization_barrier(jnp.sum(probs * dprobs, axis=-1, keepdims=True))) * (1.0 / math.sqrt(HEAD))).astype(jnp.bfloat16)
    dquery = mix('phrs,pshe->prhe', dscores, key_rows)
    dkeys = mix('phrs,prhe->pshe', dscores, query_rows)
    cosine, sine = rotary_tables(seg)
    dquery = rotate(dquery, cosine, sine, -1.0).reshape(packs * width, D)
    dkeys = rotate(dkeys, cosine, sine, -1.0).reshape(packs * width, D)
    dvalues = dvalues.reshape(packs * width, D)
    dqkv = jnp.concatenate([dquery, dkeys, dvalues], axis=1).astype(jnp.bfloat16)
    d_qkv = jnp.dot(first_normed.T, dqkv, preferred_element_type=jnp.float32)
    first_norm_gradient = jnp.dot(dqkv, wqkv.T, preferred_element_type=jnp.float32)
    first_input_gradient, first_gain_gradient, first_shift_gradient = layer_normalize_backward(first_norm_gradient, first_standardized, first_inverse_deviation, norm_pairs[0])
    second_input_gradient, second_gain_gradient, second_shift_gradient = layer_normalize_backward(second_norm_gradient, second_standardized, second_inverse_deviation, norm_pairs[2])
    grad_in = (upf + first_input_gradient + second_input_gradient).astype(jnp.bfloat16)
    d_norm = jnp.stack([first_gain_gradient, first_shift_gradient, second_gain_gradient, second_shift_gradient])
    column = lax.optimization_barrier(jnp.sum(upf, axis=0))
    d_bias = jnp.stack([lax.optimization_barrier(jnp.sum(dquery, axis=0)), lax.optimization_barrier(jnp.sum(dvalues, axis=0)), column, column])
    d_upbias = lax.optimization_barrier(jnp.sum(dhidden, axis=0))
    return (grad_in, (d_qkv, d_out, d_up, d_down, d_norm, d_bias, d_upbias))

def reference(inputs, cotangent, segments, qkv_weight, out_weight, up_weight, down_weight, norm_params, bias_params, up_bias):
    packs = TOKENS // PACK
    group = 32 if packs % 32 == 0 else packs
    blocks = packs // group
    seg_all = segments.reshape(blocks, group, PACK)
    x_all = inputs.reshape(blocks, group * PACK, D)
    c_all = cotangent.reshape(blocks, group * PACK, D)
    params = (qkv_weight, out_weight, up_weight, down_weight, norm_params, bias_params, up_bias)

    def select_layer(level):
        return tuple((piece[level] for piece in params))

    def one_block(carry, item):
        xin, cot, seg = item
        first_out, first_saved = forward(xin, seg, select_layer(0))
        second_out, second_saved = forward(first_out, seg, select_layer(1))
        middle_grad, second_grads = backward(second_saved, cot, seg, select_layer(1))
        input_grad, first_grads = backward(first_saved, middle_grad, seg, select_layer(0))
        total = tuple((acc + jnp.stack([left, right]) for acc, left, right in zip(carry, first_grads, second_grads)))
        return (total, (jnp.stack([first_out, second_out]), jnp.stack([input_grad, middle_grad])))
    init = tuple((jnp.zeros(piece.shape, jnp.float32) for piece in params))
    total, (outs, grads_in) = lax.scan(one_block, init, (x_all, c_all, seg_all))
    outs = jnp.transpose(outs, (1, 0, 2, 3)).reshape(2, TOKENS, D)
    grads_in = jnp.transpose(grads_in, (1, 0, 2, 3)).reshape(2, TOKENS, D)
    return (outs, grads_in, total[0], total[1], total[2], total[3], total[4], total[5], total[6])
```

```python
import functools
import math

import jax
import jax.numpy as jnp
from jax import lax
from jax.experimental import pallas as pl
from jax.experimental.pallas import tpu as pltpu
from jax.sharding import PartitionSpec as P

D = 768
FF = 3072
HEAD = 64
ROT = 16
PACK = 128


EPS = 1e-05
HALF_ROOT = 0.7071067811865476
INV_ROOT_TAU = 0.3989422804014327
NEGATIVE = -1e30


def shifted(value, axis, steps):
    count = lax.axis_size(axis)
    initial, last = (max(0, -steps), min(count, count - steps))
    return lax.ppermute(value, axis, [(source, source + steps) for source in range(initial, last)])


def mix(form, left, right):
    return jnp.einsum(form, left, right, preferred_element_type=jnp.float32)


def layer_normalize(input_float, norm_gain, norm_shift):
    row_mean = jnp.mean(input_float, axis=-1, keepdims=True)
    centered_input = input_float - row_mean
    inverse_deviation = lax.rsqrt(
        jnp.mean(centered_input * centered_input, axis=-1, keepdims=True) + EPS
    )
    standardized_input = centered_input * inverse_deviation
    return (
        standardized_input,
        inverse_deviation,
        (standardized_input * norm_gain + norm_shift).astype(jnp.bfloat16),
    )


def layer_normalize_backward(normed_gradient, standardized_input, inverse_deviation, norm_gain):
    standardized_gradient = normed_gradient * norm_gain
    inner_width = jnp.mean(
        standardized_gradient, axis=-1, keepdims=True
    ) + standardized_input * jnp.mean(
        standardized_gradient * standardized_input, axis=-1, keepdims=True
    )
    return (
        inverse_deviation * (standardized_gradient - inner_width),
        jnp.sum(normed_gradient * standardized_input, axis=0),
        jnp.sum(normed_gradient, axis=0),
    )


def rotary_tables(seg):
    width = seg.shape[1]
    index = jnp.arange(width, dtype=jnp.int32)[None, :]
    before = jnp.concatenate([seg[:, :1] - 1, seg[:, :-1]], axis=1)
    first = lax.cummax(jnp.where(seg != before, index, 0), axis=1)
    place = (index - first).astype(jnp.float32)
    freq = 10000.0 ** (-jnp.arange(0, ROT, 2, dtype=jnp.float32) / ROT)
    angle = place[:, :, None, None] * freq
    return (jnp.cos(angle), jnp.sin(angle))


def rotate(tensor, cosine, sine, sign):
    half = ROT // 2
    first = tensor[..., :half]
    second = tensor[..., half:ROT]
    return jnp.concatenate(
        [
            first * cosine - sign * second * sine,
            second * cosine + sign * first * sine,
            tensor[..., ROT:],
        ],
        axis=-1,
    )


def scores(query_rows, key_rows, seg):
    width = seg.shape[1]
    raw = mix("prhe,pshe->phrs", query_rows, key_rows) * (1.0 / math.sqrt(HEAD))
    index = jnp.arange(width, dtype=jnp.int32)
    causal = index[:, None] >= index[None, :]
    allowed = (seg[:, None, :, None] == seg[:, None, None, :]) & causal[None, None]
    return jnp.where(allowed, raw, NEGATIVE)


def forward(x, seg, weights):
    wqkv, wout, wup, wdown, norm_pairs, abias, upbias = weights
    packs, width = seg.shape
    shape = (packs, width, D // HEAD, HEAD)
    norm_pairs = norm_pairs.astype(jnp.float32)
    abias = abias.astype(jnp.float32)
    upbias = upbias.astype(jnp.float32)
    input_float = x.astype(jnp.float32)
    first_standardized, first_inverse_deviation, first_normed = layer_normalize(
        input_float, norm_pairs[0], norm_pairs[1]
    )
    second_standardized, second_inverse_deviation, second_normed = layer_normalize(
        input_float, norm_pairs[2], norm_pairs[3]
    )
    qkv = jnp.dot(first_normed, wqkv, preferred_element_type=jnp.float32)
    cosine, sine = rotary_tables(seg)
    query_rows = rotate((qkv[:, :D] + abias[0]).reshape(shape), cosine, sine, 1.0).astype(
        jnp.bfloat16
    )
    key_rows = rotate(qkv[:, D : 2 * D].reshape(shape), cosine, sine, 1.0).astype(jnp.bfloat16)
    value_rows = (qkv[:, 2 * D :] + abias[1]).reshape(shape).astype(jnp.bfloat16)
    raw = scores(query_rows, key_rows, seg)
    top = jnp.max(raw, axis=-1, keepdims=True)
    log_sum_exp = top + jnp.log(jnp.sum(jnp.exp(raw - top), axis=-1, keepdims=True))
    probs = jnp.exp(raw - log_sum_exp).astype(jnp.bfloat16)
    context_rows = (
        mix("phrs,pshe->prhe", probs, value_rows).reshape(packs * width, D).astype(jnp.bfloat16)
    )
    attended = jnp.dot(context_rows, wout, preferred_element_type=jnp.float32) + abias[2]
    hidden_rows = jnp.dot(second_normed, wup, preferred_element_type=jnp.float32) + upbias
    activation_output = (0.5 * hidden_rows * (1.0 + lax.erf(hidden_rows * HALF_ROOT))).astype(
        jnp.bfloat16
    )
    mlp = jnp.dot(activation_output, wdown, preferred_element_type=jnp.float32) + abias[3]
    result = (input_float + attended + mlp).astype(jnp.bfloat16)
    saved_state = (
        first_standardized,
        first_inverse_deviation,
        first_normed,
        second_standardized,
        second_inverse_deviation,
        second_normed,
        query_rows,
        key_rows,
        value_rows,
        log_sum_exp,
        context_rows,
        hidden_rows,
        activation_output,
    )
    return (result, saved_state)


def backward(saved_state, upstream, seg, weights):
    wqkv, wout, wup, wdown, norm_pairs, abias, upbias = weights
    (
        first_standardized,
        first_inverse_deviation,
        first_normed,
        second_standardized,
        second_inverse_deviation,
        second_normed,
        query_rows,
        key_rows,
        value_rows,
        log_sum_exp,
        context_rows,
        hidden_rows,
        activation_output,
    ) = saved_state
    packs, width = seg.shape
    shape = (packs, width, D // HEAD, HEAD)
    norm_pairs = norm_pairs.astype(jnp.float32)
    upf = upstream.astype(jnp.float32)
    d_down = jnp.dot(activation_output.T, upstream, preferred_element_type=jnp.float32)
    dgelu = jnp.dot(upstream, wdown.T, preferred_element_type=jnp.float32)
    slope = 0.5 * (1.0 + lax.erf(hidden_rows * HALF_ROOT)) + hidden_rows * INV_ROOT_TAU * jnp.exp(
        -0.5 * hidden_rows * hidden_rows
    )
    dhidden = dgelu * slope
    dhidden_low = dhidden.astype(jnp.bfloat16)
    d_up = jnp.dot(second_normed.T, dhidden_low, preferred_element_type=jnp.float32)
    second_norm_gradient = jnp.dot(dhidden_low, wup.T, preferred_element_type=jnp.float32)
    d_out = jnp.dot(context_rows.T, upstream, preferred_element_type=jnp.float32)
    dctx = (
        jnp.dot(upstream, wout.T, preferred_element_type=jnp.float32)
        .reshape(shape)
        .astype(jnp.bfloat16)
    )
    probs = jnp.exp(scores(query_rows, key_rows, seg) - log_sum_exp)
    dvalues = mix("phrs,prhe->pshe", probs.astype(jnp.bfloat16), dctx)
    dprobs = mix("prhe,pshe->phrs", dctx, value_rows)
    dscores = (
        probs * (dprobs - jnp.sum(probs * dprobs, axis=-1, keepdims=True)) * (1.0 / math.sqrt(HEAD))
    ).astype(jnp.bfloat16)
    dquery = mix("phrs,pshe->prhe", dscores, key_rows)
    dkeys = mix("phrs,prhe->pshe", dscores, query_rows)
    cosine, sine = rotary_tables(seg)
    dquery = rotate(dquery, cosine, sine, -1.0).reshape(packs * width, D)
    dkeys = rotate(dkeys, cosine, sine, -1.0).reshape(packs * width, D)
    dvalues = dvalues.reshape(packs * width, D)
    dqkv = jnp.concatenate([dquery, dkeys, dvalues], axis=1).astype(jnp.bfloat16)
    d_qkv = jnp.dot(first_normed.T, dqkv, preferred_element_type=jnp.float32)
    first_norm_gradient = jnp.dot(dqkv, wqkv.T, preferred_element_type=jnp.float32)
    first_input_gradient, first_gain_gradient, first_shift_gradient = layer_normalize_backward(
        first_norm_gradient, first_standardized, first_inverse_deviation, norm_pairs[0]
    )
    second_input_gradient, second_gain_gradient, second_shift_gradient = layer_normalize_backward(
        second_norm_gradient, second_standardized, second_inverse_deviation, norm_pairs[2]
    )
    grad_in = (upf + first_input_gradient + second_input_gradient).astype(jnp.bfloat16)
    d_norm = jnp.stack(
        [first_gain_gradient, first_shift_gradient, second_gain_gradient, second_shift_gradient]
    )
    column = jnp.sum(upf, axis=0)
    d_bias = jnp.stack([jnp.sum(dquery, axis=0), jnp.sum(dvalues, axis=0), column, column])
    d_upbias = jnp.sum(dhidden, axis=0)
    return (grad_in, (d_qkv, d_out, d_up, d_down, d_norm, d_bias, d_upbias))


def send_forward(result):
    return shifted(result, "section", 1)


def send_back(grad_in):
    return shifted(grad_in, "section", -1)


MESH = pl.DeviceIdType.MESH


def place_of(count):
    me = lax.axis_index("dp")
    outer = count // 4
    return me // 4, lax.rem(me // 2, 2), lax.rem(me, 2), outer


def index_of(o, m, c):
    return (o * 2 + m) * 2 + c


def greet(o, m, c, outer):
    barrier = pltpu.get_barrier_semaphore()
    peers = [index_of(lax.rem(o + r, outer), m, c) for r in range(1, outer)]
    peers += [index_of(o, 1 - m, c), index_of(o, m, 1 - c)]
    for peer in peers:
        pl.semaphore_signal(barrier, inc=1, device_id={"dp": peer}, device_id_type=MESH)
    pl.semaphore_wait(barrier, len(peers))


def remote(src, dst, send, recv, peer):
    return pltpu.make_async_remote_copy(
        src_ref=src,
        dst_ref=dst,
        send_sem=send,
        recv_sem=recv,
        device_id={"dp": peer},
        device_id_type=MESH,
    )


def gather_kernel(count, kinds, *refs):
    ins, outs = refs[:kinds], refs[kinds : 2 * kinds]
    own_sem, outer_s, outer_r, mid_s, mid_r, core_s, core_r = refs[2 * kinds :]
    o, m, c, outer = place_of(count)
    me = index_of(o, m, c)
    mid_peer, core_peer = index_of(o, 1 - m, c), index_of(o, m, 1 - c)
    greet(o, m, c, outer)
    started, locals_ = [], []

    def outer_copy(k, r):
        return remote(
            ins[k],
            outs[k].at[me],
            outer_s.at[r - 1, k],
            outer_r.at[r - 1, k],
            index_of(lax.rem(o + r, outer), m, c),
        )

    def slot(r, far):
        return index_of(lax.rem(o + outer - r, outer), (1 - m) if far else m, c)

    def mid_copy(k, r):
        src = ins[k] if r == 0 else outs[k].at[slot(r, False)]
        return remote(
            src, outs[k].at[slot(r, False)], mid_s.at[r, k], mid_r.at[r, k], mid_peer
        )

    def core_copy(k, r, far):
        src = ins[k] if r == 0 and not far else outs[k].at[slot(r, far)]
        return remote(
            src,
            outs[k].at[slot(r, far)],
            core_s.at[far, r, k],
            core_r.at[far, r, k],
            core_peer,
        )

    def begin(copy):
        copy.start()
        started.append(copy)

    for k in range(kinds):
        for r in range(1, outer):
            begin(outer_copy(k, r))
        begin(mid_copy(k, 0))
        begin(core_copy(k, 0, 0))
        local = pltpu.make_async_copy(ins[k], outs[k].at[me], own_sem.at[k])
        local.start()
        locals_.append(local)

    def pass_on(k):
        for r in range(outer):
            mid_copy(k, r).wait_recv()
            begin(core_copy(k, r, 1))

    for k in range(kinds):
        for r in range(1, outer):
            outer_copy(k, r).wait_recv()
            begin(mid_copy(k, r))
            begin(core_copy(k, r, 0))
        if k > 0:
            pass_on(k - 1)
    pass_on(kinds - 1)
    for k in range(kinds):
        for r in range(outer):
            for far in range(2):
                core_copy(k, r, far).wait_recv()
    for copy in started:
        copy.wait_send()
    for local in locals_:
        local.wait()


def gather_all(count, arrays):
    kinds, outer = len(arrays), count // 4
    anywhere = pl.BlockSpec(memory_space=pl.ANY)
    dma = pltpu.SemaphoreType.DMA
    return pl.pallas_call(
        functools.partial(gather_kernel, count, kinds),
        out_shape=[jax.ShapeDtypeStruct((count,) + a.shape, a.dtype) for a in arrays],
        in_specs=[anywhere] * kinds,
        out_specs=[anywhere] * kinds,
        scratch_shapes=[
            dma((kinds,)),
            dma((outer - 1, kinds)),
            dma((outer - 1, kinds)),
            dma((outer, kinds)),
            dma((outer, kinds)),
            dma((2, outer, kinds)),
            dma((2, outer, kinds)),
        ],
        compiler_params=pltpu.CompilerParams(collective_id=0, has_side_effects=True),
        name="gather_weights",
    )(*arrays)


def add(left, right):
    return (left.astype(jnp.float32) + right.astype(jnp.float32)).astype(left.dtype)


def scatter_kernel(count, kinds, *refs):
    ins, outs = refs[:kinds], refs[kinds : 2 * kinds]
    near, middle, last = (refs[(2 + i) * kinds : (3 + i) * kinds] for i in range(3))
    core_s, core_r, mid_s, mid_r, outer_s, outer_r = refs[5 * kinds :]
    o, m, c, outer = place_of(count)
    mid_peer, core_peer = index_of(o, 1 - m, c), index_of(o, m, 1 - c)
    greet(o, m, c, outer)
    order = list(range(1, outer)) + [0]
    started = []

    def begin(copy):
        copy.start()
        started.append(copy)

    def shard(r, far, core):
        return index_of(lax.rem(o + r, outer), (1 - m) if far else m, core)

    def core_copy(k, r, far):
        return remote(
            ins[k].at[shard(r, far, 1 - c)],
            near[k].at[far, r],
            core_s.at[far, r, k],
            core_r.at[far, r, k],
            core_peer,
        )

    def mid_copy(k, r):
        return remote(
            near[k].at[1, r], middle[k].at[r], mid_s.at[r, k], mid_r.at[r, k], mid_peer
        )

    def outer_copy(k, r):
        return remote(
            middle[k].at[r],
            last[k].at[r - 1],
            outer_s.at[r - 1, k],
            outer_r.at[r - 1, k],
            index_of(lax.rem(o + r, outer), m, c),
        )

    for far in (1, 0):
        for k in range(kinds):
            for r in order:
                begin(core_copy(k, r, far))
    for far in (1, 0):
        for k in range(kinds):
            for r in order:
                core_copy(k, r, far).wait_recv()
                near[k][far, r] = add(near[k][far, r], ins[k][shard(r, far, c)])
                if far:
                    begin(mid_copy(k, r))
    for k in range(kinds):
        for r in order:
            mid_copy(k, r).wait_recv()
            middle[k][r] = add(middle[k][r], near[k][0, r])
            if r:
                begin(outer_copy(k, r))
    for k in range(kinds):
        total = middle[k][0].astype(jnp.float32)
        for r in range(1, outer):
            outer_copy(k, r).wait_recv()
            total = total + last[k][r - 1].astype(jnp.float32)
        outs[k][...] = total
    for copy in started:
        copy.wait_send()


def scatter_all(count, arrays):
    kinds, outer = len(arrays), count // 4
    fast = pl.BlockSpec(memory_space=pltpu.VMEM)
    dma = pltpu.SemaphoreType.DMA
    return pl.pallas_call(
        functools.partial(scatter_kernel, count, kinds),
        out_shape=[jax.ShapeDtypeStruct(a.shape[1:], jnp.float32) for a in arrays],
        in_specs=[fast] * kinds,
        out_specs=[fast] * kinds,
        scratch_shapes=[pltpu.VMEM((2, outer) + a.shape[1:], a.dtype) for a in arrays]
        + [pltpu.VMEM((outer,) + a.shape[1:], a.dtype) for a in arrays]
        + [pltpu.VMEM((outer - 1,) + a.shape[1:], a.dtype) for a in arrays]
        + [
            dma((2, outer, kinds)),
            dma((2, outer, kinds)),
            dma((outer, kinds)),
            dma((outer, kinds)),
            dma((outer - 1, kinds)),
            dma((outer - 1, kinds)),
        ],
        compiler_params=pltpu.CompilerParams(
            collective_id=1, has_side_effects=True, vmem_limit_bytes=56 * 2**20
        ),
        name="scatter_gradients",
    )(*arrays)


def dense_shape(rows, columns):
    if rows % 16 == 0:
        return (rows, columns)
    return (rows * columns // 128, 128)


def on_device(
    count,
    inputs,
    cotangent,
    segments,
    qkv_weight,
    out_weight,
    up_weight,
    down_weight,
    norm_params,
    bias_params,
    up_bias,
):
    is_first = lax.axis_index("section") == 0
    large = (qkv_weight[0], out_weight[0], up_weight[0], down_weight[0])
    shapes = [dense_shape(*piece.shape) for piece in large]
    narrow = norm_params.shape[2]
    fields = (4 * narrow, 4 * narrow, up_bias.shape[1])
    used = sum(fields)
    small = jnp.concatenate(
        [norm_params[0].reshape(-1), bias_params[0].reshape(-1), up_bias[0]]
    )
    padded = -(-used // 2048) * 2048
    small = jnp.pad(small, (0, padded - used)).reshape(-1, 128)
    gathered = gather_all(
        count, [small] + [piece.reshape(shape) for piece, shape in zip(large, shapes)]
    )
    flat = gathered[0].reshape(count, padded)
    norm_all = (
        flat[:, : fields[0]].reshape(count, 4, narrow).transpose(1, 0, 2).reshape(4, D)
    )
    bias_all = (
        flat[:, fields[0] : fields[0] + fields[1]]
        .reshape(count, 4, narrow)
        .transpose(1, 0, 2)
        .reshape(4, D)
    )
    up_bias_all = flat[:, fields[0] + fields[1] : used].reshape(FF)
    weights = tuple(
        whole.reshape(count * piece.shape[0], piece.shape[1])
        for whole, piece in zip(gathered[1:], large)
    ) + (norm_all, bias_all, up_bias_all)

    seg = segments.reshape(-1, PACK)
    early, _ = forward(inputs, seg, weights)
    arrived = send_forward(early)
    layer_in = jnp.where(is_first, inputs, arrived)
    layer_out, saved_state = forward(layer_in, seg, weights)
    early_grad, _ = backward(saved_state, cotangent, seg, weights)
    returned = send_back(early_grad)
    upstream = jnp.where(is_first, returned, cotangent)
    input_grad, grads = backward(saved_state, upstream, seg, weights)

    small_grad = jnp.concatenate(
        [
            grads[4].reshape(4, count, narrow).transpose(1, 0, 2).reshape(count, -1),
            grads[5].reshape(4, count, narrow).transpose(1, 0, 2).reshape(count, -1),
            grads[6].reshape(count, -1),
        ],
        axis=1,
    )
    padded_grad = -(-used // 1024) * 1024
    small_grad = jnp.pad(small_grad, ((0, 0), (0, padded_grad - used)))
    owned = scatter_all(
        count,
        [small_grad.reshape(count, -1, 128)]
        + [
            grad.astype(jnp.bfloat16).reshape((count,) + shape)
            for grad, shape in zip(grads[:4], shapes)
        ],
    )
    tiny = owned[0].reshape(-1)
    result = [
        whole.reshape((1,) + piece.shape) for whole, piece in zip(owned[1:], large)
    ]
    return (
        layer_out[None],
        input_grad[None],
        *result,
        tiny[: fields[0]].reshape(1, 4, narrow),
        tiny[fields[0] : fields[0] + fields[1]].reshape(1, 4, narrow),
        tiny[fields[0] + fields[1] : used].reshape(1, -1),
    )


def solution(mesh):
    in_specs = (
        P("dp", None),
        P("dp", None),
        P("dp"),
        P("section", "dp", None),
        P("section", "dp", None),
        P("section", "dp", None),
        P("section", "dp", None),
        P("section", None, "dp"),
        P("section", None, "dp"),
        P("section", "dp"),
    )
    out_specs = (
        P("section", "dp", None),
        P("section", "dp", None),
        P("section", "dp", None),
        P("section", "dp", None),
        P("section", "dp", None),
        P("section", "dp", None),
        P("section", None, "dp"),
        P("section", None, "dp"),
        P("section", "dp"),
    )
    return jax.shard_map(
        functools.partial(on_device, mesh.shape["dp"]), mesh=mesh, in_specs=in_specs, out_specs=out_specs, check_vma=False
    )
```

```python
import functools
import math

import jax
import jax.numpy as jnp
from jax import lax
from jax.experimental import pallas as pl
from jax.experimental.pallas import tpu as pltpu
from jax.sharding import PartitionSpec as P

D = 768
FF = 3072
HEAD = 64
ROT = 16
PACK = 128


EPS = 1e-05
HALF_ROOT = 0.7071067811865476
INV_ROOT_TAU = 0.3989422804014327
NEGATIVE = -1e30


def shifted(value, axis, steps):
    count = lax.axis_size(axis)
    initial, last = (max(0, -steps), min(count, count - steps))
    return lax.ppermute(value, axis, [(source, source + steps) for source in range(initial, last)])


def rotary_tables(seg):
    packs, width = seg.shape
    index = jnp.arange(width, dtype=jnp.int32)[None, :]
    before = jnp.concatenate([seg[:, :1] - 1, seg[:, :-1]], axis=1)
    first = lax.cummax(jnp.where(seg != before, index, 0), axis=1)
    place = (index - first).astype(jnp.float32).reshape(packs * width, 1)
    half = ROT // 2
    lane = jnp.arange(2 * HEAD, dtype=jnp.int32)[None, :] % HEAD
    freq = 10000.0 ** (-2.0 * (lane % half).astype(jnp.float32) / ROT)
    angle = place * freq
    cosine, sine = jnp.cos(angle), jnp.sin(angle)
    keep = jnp.where(lane < ROT, cosine, 1.0)
    ahead = jnp.where(lane < half, -sine, 0.0)
    behind = jnp.where((lane >= half) & (lane < ROT), sine, 0.0)
    causal = index[0][:, None] >= index[0][None, :]
    allowed = (seg[:, :, None] == seg[:, None, :]) & causal[None]
    mask = jnp.where(allowed, 1.0, 0.0).astype(jnp.float32)
    return (keep, ahead, behind, mask)


PAIR = 2 * HEAD
PAIRS = D // PAIR
SCALE = 1.0 / math.sqrt(HEAD)


def turn(x, keep, ahead, behind):
    half = ROT // 2
    return (
        x * keep
        + pltpu.roll(x, PAIR - half, 1) * ahead
        + pltpu.roll(x, half, 1) * behind
    )


def low_lanes():
    return lax.broadcasted_iota(jnp.int32, (PACK, PAIR), 1) < HEAD


def stacked(x, low):
    zero = jnp.zeros_like(x)
    return jnp.concatenate([jnp.where(low, x, zero), jnp.where(low, zero, x)], axis=0)


def product(left, right, left_dim, right_dim):
    return lax.dot_general(
        left,
        right,
        (((left_dim,), (right_dim,)), ((), ())),
        preferred_element_type=jnp.float32,
    )


def attend_kernel(
    qkv_ref, bias_ref, keep_ref, ahead_ref, behind_ref, mask_ref, heads_ref, prob_ref, ctx_ref
):
    keep, ahead, behind = keep_ref[...], ahead_ref[...], behind_ref[...]
    allowed = mask_ref[0] > 0.0
    low = low_lanes()
    for pair in range(PAIRS):
        at = [slice(part * D + pair * PAIR, part * D + (pair + 1) * PAIR) for part in range(3)]
        query = turn(qkv_ref[:, at[0]] + bias_ref[0:1, at[0]], keep, ahead, behind)
        key = turn(qkv_ref[:, at[1]], keep, ahead, behind)
        value = qkv_ref[:, at[2]] + bias_ref[1:2, at[0]]
        query, value = query.astype(jnp.bfloat16), value.astype(jnp.bfloat16)
        key = key.astype(jnp.bfloat16)
        heads_ref[:, at[0]] = query
        heads_ref[:, at[1]] = key
        heads_ref[:, at[2]] = value
        raw = product(query, stacked(key, low), 1, 1) * SCALE
        sides = []
        for side in range(2):
            one = jnp.where(allowed, raw[:, side * PACK : (side + 1) * PACK], NEGATIVE)
            top = jnp.max(one, axis=-1, keepdims=True)
            lse = top + jnp.log(jnp.sum(jnp.exp(one - top), axis=-1, keepdims=True))
            sides.append(jnp.exp(one - lse))
        probs = jnp.concatenate(sides, axis=1)
        prob_ref[pair] = probs
        context = product(probs.astype(jnp.bfloat16), stacked(value, low), 1, 0)
        ctx_ref[:, at[0]] = context.astype(jnp.bfloat16)


def attend(qkv, abias, tables):
    rows = qkv.shape[0]
    packs = rows // PACK
    wide = pl.BlockSpec((PACK, 3 * D), lambda i: (i, 0))
    table = pl.BlockSpec((PACK, PAIR), lambda i: (i, 0))
    return pl.pallas_call(
        attend_kernel,
        grid=(packs,),
        out_shape=[
            jax.ShapeDtypeStruct((rows, 3 * D), jnp.bfloat16),
            jax.ShapeDtypeStruct((packs * PAIRS, PACK, 2 * PACK), jnp.float32),
            jax.ShapeDtypeStruct((rows, D), jnp.bfloat16),
        ],
        in_specs=[
            wide,
            pl.BlockSpec((4, D), lambda i: (0, 0)),
            table,
            table,
            table,
            pl.BlockSpec((1, PACK, PACK), lambda i: (i, 0, 0)),
        ],
        out_specs=[
            wide,
            pl.BlockSpec((PAIRS, PACK, 2 * PACK), lambda i: (i, 0, 0)),
            pl.BlockSpec((PACK, D), lambda i: (i, 0)),
        ],
        compiler_params=pltpu.CompilerParams(vmem_limit_bytes=32 * 2**20),
        name="attend",
    )(qkv, abias, *tables)


def attend_back_kernel(
    heads_ref, prob_ref, dctx_ref, keep_ref, ahead_ref, behind_ref, dqkv_ref, sums_ref
):
    keep, ahead, behind = keep_ref[...], -ahead_ref[...], -behind_ref[...]
    low = low_lanes()
    for pair in range(PAIRS):
        at = [slice(part * D + pair * PAIR, part * D + (pair + 1) * PAIR) for part in range(3)]
        query, key, value = (heads_ref[:, at[part]] for part in range(3))
        dctx = dctx_ref[:, at[0]]
        probs = prob_ref[pair]
        dvalue = product(probs.astype(jnp.bfloat16), dctx, 0, 0)
        dvalue = jnp.where(low, dvalue[:PACK], dvalue[PACK:])
        dprobs = product(dctx, stacked(value, low), 1, 1)
        sides = []
        for side in range(2):
            span = slice(side * PACK, (side + 1) * PACK)
            p, dp = probs[:, span], dprobs[:, span]
            inner = jnp.sum(p * dp, axis=-1, keepdims=True)
            sides.append((p * (dp - inner) * SCALE).astype(jnp.bfloat16))
        dscores = jnp.concatenate(sides, axis=1)
        dquery = product(dscores, stacked(key, low), 1, 0)
        dkey = product(dscores, query, 0, 0)
        dkey = jnp.where(low, dkey[:PACK], dkey[PACK:])
        dquery = turn(dquery, keep, ahead, behind)
        dkey = turn(dkey, keep, ahead, behind)
        dqkv_ref[:, at[0]] = dquery.astype(jnp.bfloat16)
        dqkv_ref[:, at[1]] = dkey.astype(jnp.bfloat16)
        dqkv_ref[:, at[2]] = dvalue.astype(jnp.bfloat16)
        sums_ref[0, 0:1, at[0]] = jnp.sum(dquery, axis=0, keepdims=True)
        sums_ref[0, 1:2, at[0]] = jnp.sum(dvalue, axis=0, keepdims=True)


def attend_back(heads, probs, dctx, tables):
    rows = heads.shape[0]
    packs = rows // PACK
    wide = pl.BlockSpec((PACK, 3 * D), lambda i: (i, 0))
    table = pl.BlockSpec((PACK, PAIR), lambda i: (i, 0))
    return pl.pallas_call(
        attend_back_kernel,
        grid=(packs,),
        out_shape=[
            jax.ShapeDtypeStruct((rows, 3 * D), jnp.bfloat16),
            jax.ShapeDtypeStruct((packs, 2, D), jnp.float32),
        ],
        in_specs=[
            wide,
            pl.BlockSpec((PAIRS, PACK, 2 * PACK), lambda i: (i, 0, 0)),
            pl.BlockSpec((PACK, D), lambda i: (i, 0)),
            table,
            table,
            table,
        ],
        out_specs=[wide, pl.BlockSpec((1, 2, D), lambda i: (i, 0, 0))],
        compiler_params=pltpu.CompilerParams(vmem_limit_bytes=32 * 2**20),
        name="attend_back",
    )(heads, probs, dctx, *tables[:3])


def forward(x, tables, weights):
    wqkv, wout, wup, wdown, norm_pairs, abias, upbias = weights
    norm_pairs = norm_pairs.astype(jnp.float32)
    abias = abias.astype(jnp.float32)
    upbias = upbias.astype(jnp.float32)
    input_float = x.astype(jnp.float32)
    row_mean = jnp.mean(input_float, axis=-1, keepdims=True)
    centered = input_float - row_mean
    inverse_deviation = lax.rsqrt(jnp.mean(centered * centered, axis=-1, keepdims=True) + EPS)
    standardized = centered * inverse_deviation
    first_normed = (standardized * norm_pairs[0] + norm_pairs[1]).astype(jnp.bfloat16)
    second_normed = (standardized * norm_pairs[2] + norm_pairs[3]).astype(jnp.bfloat16)
    qkv = jnp.dot(first_normed, wqkv, preferred_element_type=jnp.float32)
    heads, probs, context_rows = attend(qkv, abias, tables)
    attended = jnp.dot(context_rows, wout, preferred_element_type=jnp.float32) + abias[2]
    hidden_rows = jnp.dot(second_normed, wup, preferred_element_type=jnp.float32) + upbias
    activation_output = (0.5 * hidden_rows * (1.0 + lax.erf(hidden_rows * HALF_ROOT))).astype(
        jnp.bfloat16
    )
    mlp = jnp.dot(activation_output, wdown, preferred_element_type=jnp.float32) + abias[3]
    result = (input_float + attended + mlp).astype(jnp.bfloat16)
    saved_state = (
        standardized,
        inverse_deviation,
        first_normed,
        second_normed,
        heads,
        probs,
        context_rows,
        hidden_rows,
        activation_output,
    )
    return (result, saved_state)


def backward(saved_state, upstream, tables, weights):
    wqkv, wout, wup, wdown, norm_pairs, abias, upbias = weights
    (
        standardized,
        inverse_deviation,
        first_normed,
        second_normed,
        heads,
        probs,
        context_rows,
        hidden_rows,
        activation_output,
    ) = saved_state
    norm_pairs = norm_pairs.astype(jnp.float32)
    upf = upstream.astype(jnp.float32)
    dctx = product(upstream, wout, 1, 1).astype(jnp.bfloat16)
    dqkv, sums = attend_back(heads, probs, dctx, tables)
    d_down = product(activation_output, upstream, 0, 0)
    dgelu = product(upstream, wdown, 1, 1)
    slope = 0.5 * (1.0 + lax.erf(hidden_rows * HALF_ROOT)) + hidden_rows * INV_ROOT_TAU * jnp.exp(
        -0.5 * hidden_rows * hidden_rows
    )
    dhidden = dgelu * slope
    dhidden_low = dhidden.astype(jnp.bfloat16)
    d_up = product(second_normed, dhidden_low, 0, 0)
    second_gradient = product(dhidden_low, wup, 1, 1)
    d_out = product(context_rows, upstream, 0, 0)
    d_qkv = product(first_normed, dqkv, 0, 0)
    first_gradient = product(dqkv, wqkv, 1, 1)
    inner = first_gradient * norm_pairs[0] + second_gradient * norm_pairs[2]
    input_gradient = inverse_deviation * (
        inner
        - jnp.mean(inner, axis=-1, keepdims=True)
        - standardized * jnp.mean(inner * standardized, axis=-1, keepdims=True)
    )
    grad_in = (upf + input_gradient).astype(jnp.bfloat16)
    d_norm = jnp.stack(
        [
            jnp.sum(first_gradient * standardized, axis=0),
            jnp.sum(first_gradient, axis=0),
            jnp.sum(second_gradient * standardized, axis=0),
            jnp.sum(second_gradient, axis=0),
        ]
    )
    column = jnp.sum(upf, axis=0)
    pair = jnp.sum(sums, axis=0)
    d_bias = jnp.stack([pair[0], pair[1], column, column])
    d_upbias = jnp.sum(dhidden, axis=0)
    return (grad_in, (d_qkv, d_out, d_up, d_down, d_norm, d_bias, d_upbias))


def send_forward(result):
    return shifted(result, "section", 1)


def send_back(grad_in):
    return shifted(grad_in, "section", -1)


MESH = pl.DeviceIdType.MESH


def place_of(count):
    me = lax.axis_index("dp")
    outer = count // 4
    return me // 4, lax.rem(me // 2, 2), lax.rem(me, 2), outer


def index_of(o, m, c):
    return (o * 2 + m) * 2 + c


def greet(o, m, c, outer):
    barrier = pltpu.get_barrier_semaphore()
    peers = [index_of(lax.rem(o + r, outer), m, c) for r in range(1, outer)]
    peers += [index_of(o, 1 - m, c), index_of(o, m, 1 - c)]
    for peer in peers:
        pl.semaphore_signal(barrier, inc=1, device_id={"dp": peer}, device_id_type=MESH)
    pl.semaphore_wait(barrier, len(peers))


def remote(src, dst, send, recv, peer):
    return pltpu.make_async_remote_copy(
        src_ref=src,
        dst_ref=dst,
        send_sem=send,
        recv_sem=recv,
        device_id={"dp": peer},
        device_id_type=MESH,
    )


def gather_kernel(count, kinds, *refs):
    ins, outs = refs[:kinds], refs[kinds : 2 * kinds]
    own_sem, outer_s, outer_r, mid_s, mid_r, core_s, core_r = refs[2 * kinds :]
    o, m, c, outer = place_of(count)
    me = index_of(o, m, c)
    mid_peer, core_peer = index_of(o, 1 - m, c), index_of(o, m, 1 - c)
    greet(o, m, c, outer)
    started, locals_ = [], []

    def outer_copy(k, r):
        return remote(
            ins[k],
            outs[k].at[me],
            outer_s.at[r - 1, k],
            outer_r.at[r - 1, k],
            index_of(lax.rem(o + r, outer), m, c),
        )

    def slot(r, far):
        return index_of(lax.rem(o + outer - r, outer), (1 - m) if far else m, c)

    def mid_copy(k, r):
        src = ins[k] if r == 0 else outs[k].at[slot(r, False)]
        return remote(
            src, outs[k].at[slot(r, False)], mid_s.at[r, k], mid_r.at[r, k], mid_peer
        )

    def core_copy(k, r, far):
        src = ins[k] if r == 0 and not far else outs[k].at[slot(r, far)]
        return remote(
            src,
            outs[k].at[slot(r, far)],
            core_s.at[far, r, k],
            core_r.at[far, r, k],
            core_peer,
        )

    def begin(copy):
        copy.start()
        started.append(copy)

    for k in range(kinds):
        for r in range(1, outer):
            begin(outer_copy(k, r))
        begin(mid_copy(k, 0))
        begin(core_copy(k, 0, 0))
        local = pltpu.make_async_copy(ins[k], outs[k].at[me], own_sem.at[k])
        local.start()
        locals_.append(local)

    def pass_on(k):
        for r in range(outer):
            mid_copy(k, r).wait_recv()
            begin(core_copy(k, r, 1))

    for k in range(kinds):
        for r in range(1, outer):
            outer_copy(k, r).wait_recv()
            begin(mid_copy(k, r))
            begin(core_copy(k, r, 0))
        if k > 0:
            pass_on(k - 1)
    pass_on(kinds - 1)
    for k in range(kinds):
        for r in range(outer):
            for far in range(2):
                core_copy(k, r, far).wait_recv()
    for copy in started:
        copy.wait_send()
    for local in locals_:
        local.wait()


def gather_all(count, arrays):
    kinds, outer = len(arrays), count // 4
    anywhere = pl.BlockSpec(memory_space=pl.ANY)
    dma = pltpu.SemaphoreType.DMA
    return pl.pallas_call(
        functools.partial(gather_kernel, count, kinds),
        out_shape=[jax.ShapeDtypeStruct((count,) + a.shape, a.dtype) for a in arrays],
        in_specs=[anywhere] * kinds,
        out_specs=[anywhere] * kinds,
        scratch_shapes=[
            dma((kinds,)),
            dma((outer - 1, kinds)),
            dma((outer - 1, kinds)),
            dma((outer, kinds)),
            dma((outer, kinds)),
            dma((2, outer, kinds)),
            dma((2, outer, kinds)),
        ],
        compiler_params=pltpu.CompilerParams(collective_id=0, has_side_effects=True),
        name="gather_weights",
    )(*arrays)


def add(left, right):
    return (left.astype(jnp.float32) + right.astype(jnp.float32)).astype(left.dtype)


def scatter_kernel(count, kinds, *refs):
    ins, outs = refs[:kinds], refs[kinds : 2 * kinds]
    near, middle, last = (refs[(2 + i) * kinds : (3 + i) * kinds] for i in range(3))
    core_s, core_r, mid_s, mid_r, outer_s, outer_r = refs[5 * kinds :]
    o, m, c, outer = place_of(count)
    mid_peer, core_peer = index_of(o, 1 - m, c), index_of(o, m, 1 - c)
    greet(o, m, c, outer)
    order = list(range(1, outer)) + [0]
    started = []

    def begin(copy):
        copy.start()
        started.append(copy)

    def shard(r, far, core):
        return index_of(lax.rem(o + r, outer), (1 - m) if far else m, core)

    def core_copy(k, r, far):
        return remote(
            ins[k].at[shard(r, far, 1 - c)],
            near[k].at[far, r],
            core_s.at[far, r, k],
            core_r.at[far, r, k],
            core_peer,
        )

    def mid_copy(k, r):
        return remote(
            near[k].at[1, r], middle[k].at[r], mid_s.at[r, k], mid_r.at[r, k], mid_peer
        )

    def outer_copy(k, r):
        return remote(
            middle[k].at[r],
            last[k].at[r - 1],
            outer_s.at[r - 1, k],
            outer_r.at[r - 1, k],
            index_of(lax.rem(o + r, outer), m, c),
        )

    for far in (1, 0):
        for k in range(kinds):
            for r in order:
                begin(core_copy(k, r, far))
    for far in (1, 0):
        for k in range(kinds):
            for r in order:
                core_copy(k, r, far).wait_recv()
                near[k][far, r] = add(near[k][far, r], ins[k][shard(r, far, c)])
                if far:
                    begin(mid_copy(k, r))
    for k in range(kinds):
        for r in order:
            mid_copy(k, r).wait_recv()
            middle[k][r] = add(middle[k][r], near[k][0, r])
            if r:
                begin(outer_copy(k, r))
    for k in range(kinds):
        total = middle[k][0].astype(jnp.float32)
        for r in range(1, outer):
            outer_copy(k, r).wait_recv()
            total = total + last[k][r - 1].astype(jnp.float32)
        outs[k][...] = total
    for copy in started:
        copy.wait_send()


def scatter_all(count, arrays):
    kinds, outer = len(arrays), count // 4
    fast = pl.BlockSpec(memory_space=pltpu.VMEM)
    dma = pltpu.SemaphoreType.DMA
    return pl.pallas_call(
        functools.partial(scatter_kernel, count, kinds),
        out_shape=[jax.ShapeDtypeStruct(a.shape[1:], jnp.float32) for a in arrays],
        in_specs=[fast] * kinds,
        out_specs=[fast] * kinds,
        scratch_shapes=[pltpu.VMEM((2, outer) + a.shape[1:], a.dtype) for a in arrays]
        + [pltpu.VMEM((outer,) + a.shape[1:], a.dtype) for a in arrays]
        + [pltpu.VMEM((outer - 1,) + a.shape[1:], a.dtype) for a in arrays]
        + [
            dma((2, outer, kinds)),
            dma((2, outer, kinds)),
            dma((outer, kinds)),
            dma((outer, kinds)),
            dma((outer - 1, kinds)),
            dma((outer - 1, kinds)),
        ],
        compiler_params=pltpu.CompilerParams(
            collective_id=1, has_side_effects=True, vmem_limit_bytes=56 * 2**20
        ),
        name="scatter_gradients",
    )(*arrays)


def dense_shape(rows, columns):
    if rows % 16 == 0:
        return (rows, columns)
    return (rows * columns // 128, 128)


def on_device(
    count,
    inputs,
    cotangent,
    segments,
    qkv_weight,
    out_weight,
    up_weight,
    down_weight,
    norm_params,
    bias_params,
    up_bias,
):
    is_first = lax.axis_index("section") == 0
    large = (qkv_weight[0], out_weight[0], up_weight[0], down_weight[0])
    shapes = [dense_shape(*piece.shape) for piece in large]
    narrow = norm_params.shape[2]
    fields = (4 * narrow, 4 * narrow, up_bias.shape[1])
    used = sum(fields)
    small = jnp.concatenate(
        [norm_params[0].reshape(-1), bias_params[0].reshape(-1), up_bias[0]]
    )
    padded = -(-used // 2048) * 2048
    small = jnp.pad(small, (0, padded - used)).reshape(-1, 128)
    gathered = gather_all(
        count, [small] + [piece.reshape(shape) for piece, shape in zip(large, shapes)]
    )
    flat = gathered[0].reshape(count, padded)
    norm_all = (
        flat[:, : fields[0]].reshape(count, 4, narrow).transpose(1, 0, 2).reshape(4, D)
    )
    bias_all = (
        flat[:, fields[0] : fields[0] + fields[1]]
        .reshape(count, 4, narrow)
        .transpose(1, 0, 2)
        .reshape(4, D)
    )
    up_bias_all = flat[:, fields[0] + fields[1] : used].reshape(FF)
    weights = tuple(
        whole.reshape(count * piece.shape[0], piece.shape[1])
        for whole, piece in zip(gathered[1:], large)
    ) + (norm_all, bias_all, up_bias_all)

    seg = segments.reshape(-1, PACK)
    tables = rotary_tables(seg)
    early, _ = forward(inputs, tables, weights)
    arrived = send_forward(early)
    layer_in = jnp.where(is_first, inputs, arrived)
    layer_out, saved_state = forward(layer_in, tables, weights)
    early_grad, _ = backward(saved_state, cotangent, tables, weights)
    returned = send_back(early_grad)
    upstream = jnp.where(is_first, returned, cotangent)
    input_grad, grads = backward(saved_state, upstream, tables, weights)

    small_grad = jnp.concatenate(
        [
            grads[4].reshape(4, count, narrow).transpose(1, 0, 2).reshape(count, -1),
            grads[5].reshape(4, count, narrow).transpose(1, 0, 2).reshape(count, -1),
            grads[6].reshape(count, -1),
        ],
        axis=1,
    )
    padded_grad = -(-used // 1024) * 1024
    small_grad = jnp.pad(small_grad, ((0, 0), (0, padded_grad - used)))
    owned = scatter_all(
        count,
        [small_grad.reshape(count, -1, 128)]
        + [
            grad.astype(jnp.bfloat16).reshape((count,) + shape)
            for grad, shape in zip(grads[:4], shapes)
        ],
    )
    tiny = owned[0].reshape(-1)
    result = [
        whole.reshape((1,) + piece.shape) for whole, piece in zip(owned[1:], large)
    ]
    return (
        layer_out[None],
        input_grad[None],
        *result,
        tiny[: fields[0]].reshape(1, 4, narrow),
        tiny[fields[0] : fields[0] + fields[1]].reshape(1, 4, narrow),
        tiny[fields[0] + fields[1] : used].reshape(1, -1),
    )


def solution(mesh):
    in_specs = (
        P("dp", None),
        P("dp", None),
        P("dp"),
        P("section", "dp", None),
        P("section", "dp", None),
        P("section", "dp", None),
        P("section", "dp", None),
        P("section", None, "dp"),
        P("section", None, "dp"),
        P("section", "dp"),
    )
    out_specs = (
        P("section", "dp", None),
        P("section", "dp", None),
        P("section", "dp", None),
        P("section", "dp", None),
        P("section", "dp", None),
        P("section", "dp", None),
        P("section", None, "dp"),
        P("section", None, "dp"),
        P("section", "dp"),
    )
    return jax.shard_map(
        functools.partial(on_device, mesh.shape["dp"]), mesh=mesh, in_specs=in_specs, out_specs=out_specs, check_vma=False
    )
```

```python
import functools
import math

import jax
import jax.numpy as jnp
from jax import lax
from jax.experimental import pallas as pl
from jax.experimental.pallas import tpu as pltpu
from jax.sharding import PartitionSpec as P

D = 768
FF = 3072
HEAD = 64
ROT = 16
PACK = 128


EPS = 1e-05
HALF_ROOT = 0.7071067811865476
INV_ROOT_TAU = 0.3989422804014327
NEGATIVE = -1e30


def shifted(value, axis, steps):
    count = lax.axis_size(axis)
    initial, last = (max(0, -steps), min(count, count - steps))
    return lax.ppermute(value, axis, [(source, source + steps) for source in range(initial, last)])


def rotary_tables(seg):
    packs, width = seg.shape
    index = jnp.arange(width, dtype=jnp.int32)[None, :]
    before = jnp.concatenate([seg[:, :1] - 1, seg[:, :-1]], axis=1)
    first = lax.cummax(jnp.where(seg != before, index, 0), axis=1)
    place = (index - first).astype(jnp.float32).reshape(packs * width, 1)
    half = ROT // 2
    lane = jnp.arange(2 * HEAD, dtype=jnp.int32)[None, :] % HEAD
    freq = 10000.0 ** (-2.0 * (lane % half).astype(jnp.float32) / ROT)
    angle = place * freq
    cosine, sine = jnp.cos(angle), jnp.sin(angle)
    keep = jnp.where(lane < ROT, cosine, 1.0)
    ahead = jnp.where(lane < half, -sine, 0.0)
    behind = jnp.where((lane >= half) & (lane < ROT), sine, 0.0)
    causal = index[0][:, None] >= index[0][None, :]
    allowed = (seg[:, :, None] == seg[:, None, :]) & causal[None]
    mask = jnp.where(allowed, 1.0, 0.0).astype(jnp.float32)
    return (keep, ahead, behind, mask)


PAIR = 2 * HEAD
PAIRS = D // PAIR
SCALE = 1.0 / math.sqrt(HEAD)


def turn(x, keep, ahead, behind):
    half = ROT // 2
    return (
        x * keep
        + pltpu.roll(x, PAIR - half, 1) * ahead
        + pltpu.roll(x, half, 1) * behind
    )


def low_lanes():
    return lax.broadcasted_iota(jnp.int32, (PACK, PAIR), 1) < HEAD


def stacked(x, low):
    zero = jnp.zeros_like(x)
    return jnp.concatenate([jnp.where(low, x, zero), jnp.where(low, zero, x)], axis=0)


def product(left, right, left_dim, right_dim):
    return lax.dot_general(
        left,
        right,
        (((left_dim,), (right_dim,)), ((), ())),
        preferred_element_type=jnp.float32,
    )


def attend_kernel(
    qkv_ref, bias_ref, keep_ref, ahead_ref, behind_ref, mask_ref, heads_ref, prob_ref, ctx_ref
):
    keep, ahead, behind = keep_ref[...], ahead_ref[...], behind_ref[...]
    allowed = mask_ref[0] > 0.0
    low = low_lanes()
    for pair in range(PAIRS):
        at = [slice(part * D + pair * PAIR, part * D + (pair + 1) * PAIR) for part in range(3)]
        query = turn(qkv_ref[:, at[0]] + bias_ref[0:1, at[0]], keep, ahead, behind)
        key = turn(qkv_ref[:, at[1]], keep, ahead, behind)
        value = qkv_ref[:, at[2]] + bias_ref[1:2, at[0]]
        query, value = query.astype(jnp.bfloat16), value.astype(jnp.bfloat16)
        key = key.astype(jnp.bfloat16)
        heads_ref[:, at[0]] = query
        heads_ref[:, at[1]] = key
        heads_ref[:, at[2]] = value
        raw = product(query, stacked(key, low), 1, 1) * SCALE
        sides = []
        for side in range(2):
            one = jnp.where(allowed, raw[:, side * PACK : (side + 1) * PACK], NEGATIVE)
            top = jnp.max(one, axis=-1, keepdims=True)
            lse = top + jnp.log(jnp.sum(jnp.exp(one - top), axis=-1, keepdims=True))
            sides.append(jnp.exp(one - lse))
        probs = jnp.concatenate(sides, axis=1)
        prob_ref[pair] = probs
        context = product(probs.astype(jnp.bfloat16), stacked(value, low), 1, 0)
        ctx_ref[:, at[0]] = context.astype(jnp.bfloat16)


def attend(qkv, abias, tables):
    rows = qkv.shape[0]
    packs = rows // PACK
    wide = pl.BlockSpec((PACK, 3 * D), lambda i: (i, 0))
    table = pl.BlockSpec((PACK, PAIR), lambda i: (i, 0))
    return pl.pallas_call(
        attend_kernel,
        grid=(packs,),
        out_shape=[
            jax.ShapeDtypeStruct((rows, 3 * D), jnp.bfloat16),
            jax.ShapeDtypeStruct((packs * PAIRS, PACK, 2 * PACK), jnp.float32),
            jax.ShapeDtypeStruct((rows, D), jnp.bfloat16),
        ],
        in_specs=[
            wide,
            pl.BlockSpec((4, D), lambda i: (0, 0)),
            table,
            table,
            table,
            pl.BlockSpec((1, PACK, PACK), lambda i: (i, 0, 0)),
        ],
        out_specs=[
            wide,
            pl.BlockSpec((PAIRS, PACK, 2 * PACK), lambda i: (i, 0, 0)),
            pl.BlockSpec((PACK, D), lambda i: (i, 0)),
        ],
        compiler_params=pltpu.CompilerParams(vmem_limit_bytes=32 * 2**20),
        name="attend",
    )(qkv, abias, *tables)


def attend_back_kernel(
    heads_ref, prob_ref, dctx_ref, keep_ref, ahead_ref, behind_ref, dqkv_ref, sums_ref
):
    keep, ahead, behind = keep_ref[...], -ahead_ref[...], -behind_ref[...]
    low = low_lanes()
    for pair in range(PAIRS):
        at = [slice(part * D + pair * PAIR, part * D + (pair + 1) * PAIR) for part in range(3)]
        query, key, value = (heads_ref[:, at[part]] for part in range(3))
        dctx = dctx_ref[:, at[0]]
        probs = prob_ref[pair]
        dvalue = product(probs.astype(jnp.bfloat16), dctx, 0, 0)
        dvalue = jnp.where(low, dvalue[:PACK], dvalue[PACK:])
        dprobs = product(dctx, stacked(value, low), 1, 1)
        sides = []
        for side in range(2):
            span = slice(side * PACK, (side + 1) * PACK)
            p, dp = probs[:, span], dprobs[:, span]
            inner = jnp.sum(p * dp, axis=-1, keepdims=True)
            sides.append((p * (dp - inner) * SCALE).astype(jnp.bfloat16))
        dscores = jnp.concatenate(sides, axis=1)
        dquery = product(dscores, stacked(key, low), 1, 0)
        dkey = product(dscores, query, 0, 0)
        dkey = jnp.where(low, dkey[:PACK], dkey[PACK:])
        dquery = turn(dquery, keep, ahead, behind)
        dkey = turn(dkey, keep, ahead, behind)
        dqkv_ref[:, at[0]] = dquery.astype(jnp.bfloat16)
        dqkv_ref[:, at[1]] = dkey.astype(jnp.bfloat16)
        dqkv_ref[:, at[2]] = dvalue.astype(jnp.bfloat16)
        sums_ref[0, 0:1, at[0]] = jnp.sum(dquery, axis=0, keepdims=True)
        sums_ref[0, 1:2, at[0]] = jnp.sum(dvalue, axis=0, keepdims=True)


def attend_back(heads, probs, dctx, tables):
    rows = heads.shape[0]
    packs = rows // PACK
    wide = pl.BlockSpec((PACK, 3 * D), lambda i: (i, 0))
    table = pl.BlockSpec((PACK, PAIR), lambda i: (i, 0))
    return pl.pallas_call(
        attend_back_kernel,
        grid=(packs,),
        out_shape=[
            jax.ShapeDtypeStruct((rows, 3 * D), jnp.bfloat16),
            jax.ShapeDtypeStruct((packs, 2, D), jnp.float32),
        ],
        in_specs=[
            wide,
            pl.BlockSpec((PAIRS, PACK, 2 * PACK), lambda i: (i, 0, 0)),
            pl.BlockSpec((PACK, D), lambda i: (i, 0)),
            table,
            table,
            table,
        ],
        out_specs=[wide, pl.BlockSpec((1, 2, D), lambda i: (i, 0, 0))],
        compiler_params=pltpu.CompilerParams(vmem_limit_bytes=32 * 2**20),
        name="attend_back",
    )(heads, probs, dctx, *tables[:3])


def forward(x, tables, weights):
    wqkv, wout, wup, wdown, norm_pairs, abias, upbias = weights
    norm_pairs = norm_pairs.astype(jnp.float32)
    abias = abias.astype(jnp.float32)
    upbias = upbias.astype(jnp.float32)
    input_float = x.astype(jnp.float32)
    row_mean = jnp.mean(input_float, axis=-1, keepdims=True)
    centered = input_float - row_mean
    inverse_deviation = lax.rsqrt(jnp.mean(centered * centered, axis=-1, keepdims=True) + EPS)
    standardized = centered * inverse_deviation
    first_normed = (standardized * norm_pairs[0] + norm_pairs[1]).astype(jnp.bfloat16)
    second_normed = (standardized * norm_pairs[2] + norm_pairs[3]).astype(jnp.bfloat16)
    qkv = jnp.dot(first_normed, wqkv, preferred_element_type=jnp.float32)
    heads, probs, context_rows = attend(qkv, abias, tables)
    attended = jnp.dot(context_rows, wout, preferred_element_type=jnp.float32) + abias[2]
    hidden_rows = jnp.dot(second_normed, wup, preferred_element_type=jnp.float32) + upbias
    activation_output = (0.5 * hidden_rows * (1.0 + lax.erf(hidden_rows * HALF_ROOT))).astype(
        jnp.bfloat16
    )
    mlp = jnp.dot(activation_output, wdown, preferred_element_type=jnp.float32) + abias[3]
    result = (input_float + attended + mlp).astype(jnp.bfloat16)
    saved_state = (
        standardized,
        inverse_deviation,
        first_normed,
        second_normed,
        heads,
        probs,
        context_rows,
        hidden_rows,
        activation_output,
    )
    return (result, saved_state)


def backward(saved_state, upstream, tables, weights):
    wqkv, wout, wup, wdown, norm_pairs, abias, upbias = weights
    (
        standardized,
        inverse_deviation,
        first_normed,
        second_normed,
        heads,
        probs,
        context_rows,
        hidden_rows,
        activation_output,
    ) = saved_state
    norm_pairs = norm_pairs.astype(jnp.float32)
    upf = upstream.astype(jnp.float32)
    dctx = product(upstream, wout, 1, 1).astype(jnp.bfloat16)
    dqkv, sums = attend_back(heads, probs, dctx, tables)
    d_down = product(activation_output, upstream, 0, 0)
    dgelu = product(upstream, wdown, 1, 1)
    slope = 0.5 * (1.0 + lax.erf(hidden_rows * HALF_ROOT)) + hidden_rows * INV_ROOT_TAU * jnp.exp(
        -0.5 * hidden_rows * hidden_rows
    )
    dhidden = dgelu * slope
    dhidden_low = dhidden.astype(jnp.bfloat16)
    d_up = product(second_normed, dhidden_low, 0, 0)
    second_gradient = product(dhidden_low, wup, 1, 1)
    d_out = product(context_rows, upstream, 0, 0)
    d_qkv = product(first_normed, dqkv, 0, 0)
    first_gradient = product(dqkv, wqkv, 1, 1)
    inner = first_gradient * norm_pairs[0] + second_gradient * norm_pairs[2]
    input_gradient = inverse_deviation * (
        inner
        - jnp.mean(inner, axis=-1, keepdims=True)
        - standardized * jnp.mean(inner * standardized, axis=-1, keepdims=True)
    )
    grad_in = (upf + input_gradient).astype(jnp.bfloat16)
    d_norm = jnp.stack(
        [
            jnp.sum(first_gradient * standardized, axis=0),
            jnp.sum(first_gradient, axis=0),
            jnp.sum(second_gradient * standardized, axis=0),
            jnp.sum(second_gradient, axis=0),
        ]
    )
    column = jnp.sum(upf, axis=0)
    pair = jnp.sum(sums, axis=0)
    d_bias = jnp.stack([pair[0], pair[1], column, column])
    d_upbias = jnp.sum(dhidden, axis=0)
    return (grad_in, (d_qkv, d_out, d_up, d_down, d_norm, d_bias, d_upbias))


def send_forward(result):
    return shifted(result, "section", 1)


def send_back(grad_in):
    return shifted(grad_in, "section", -1)


MESH = pl.DeviceIdType.MESH


def place_of(count):
    me = lax.axis_index("dp")
    outer = count // 4
    return me // 4, lax.rem(me // 2, 2), lax.rem(me, 2), outer


def index_of(o, m, c):
    return (o * 2 + m) * 2 + c


def greet(o, m, c, outer):
    barrier = pltpu.get_barrier_semaphore()
    peers = [index_of(lax.rem(o + r, outer), m, c) for r in range(1, outer)]
    peers += [index_of(o, 1 - m, c), index_of(o, m, 1 - c)]
    for peer in peers:
        pl.semaphore_signal(barrier, inc=1, device_id={"dp": peer}, device_id_type=MESH)
    pl.semaphore_wait(barrier, len(peers))


def remote(src, dst, send, recv, peer):
    return pltpu.make_async_remote_copy(
        src_ref=src,
        dst_ref=dst,
        send_sem=send,
        recv_sem=recv,
        device_id={"dp": peer},
        device_id_type=MESH,
    )


def gather_kernel(count, kinds, *refs):
    ins, outs = refs[:kinds], refs[kinds : 2 * kinds]
    own_sem, outer_s, outer_r, mid_s, mid_r, core_s, core_r = refs[2 * kinds :]
    o, m, c, outer = place_of(count)
    me = index_of(o, m, c)
    mid_peer, core_peer = index_of(o, 1 - m, c), index_of(o, m, 1 - c)
    greet(o, m, c, outer)
    started, locals_ = [], []

    def outer_copy(k, r):
        return remote(
            ins[k],
            outs[k].at[me],
            outer_s.at[r - 1, k],
            outer_r.at[r - 1, k],
            index_of(lax.rem(o + r, outer), m, c),
        )

    def slot(r, far):
        return index_of(lax.rem(o + outer - r, outer), (1 - m) if far else m, c)

    def mid_copy(k, r):
        src = ins[k] if r == 0 else outs[k].at[slot(r, False)]
        return remote(
            src, outs[k].at[slot(r, False)], mid_s.at[r, k], mid_r.at[r, k], mid_peer
        )

    def core_copy(k, r, far):
        src = ins[k] if r == 0 and not far else outs[k].at[slot(r, far)]
        return remote(
            src,
            outs[k].at[slot(r, far)],
            core_s.at[far, r, k],
            core_r.at[far, r, k],
            core_peer,
        )

    def begin(copy):
        copy.start()
        started.append(copy)

    for k in range(kinds):
        for r in range(1, outer):
            begin(outer_copy(k, r))
        begin(mid_copy(k, 0))
        begin(core_copy(k, 0, 0))
        local = pltpu.make_async_copy(ins[k], outs[k].at[me], own_sem.at[k])
        local.start()
        locals_.append(local)

    def pass_on(k):
        for r in range(outer):
            mid_copy(k, r).wait_recv()
            begin(core_copy(k, r, 1))

    for k in range(kinds):
        for r in range(1, outer):
            outer_copy(k, r).wait_recv()
            begin(mid_copy(k, r))
            begin(core_copy(k, r, 0))
        if k > 0:
            pass_on(k - 1)
    pass_on(kinds - 1)
    for k in range(kinds):
        for r in range(outer):
            for far in range(2):
                core_copy(k, r, far).wait_recv()
    for copy in started:
        copy.wait_send()
    for local in locals_:
        local.wait()


def gather_line_kernel(count, kinds, mid_first, *refs):
    ins, outs = refs[:kinds], refs[kinds : 2 * kinds]
    own_sem, line_s, line_r, mid_s, mid_r, core_s, core_r = refs[2 * kinds :]
    o, m, c, outer = place_of(count)
    mid_peer, core_peer = index_of(o, 1 - m, c), index_of(o, m, 1 - c)
    greet(o, m, c, outer)
    late = [k for k in range(kinds) if k in mid_first]
    order = [k for k in range(kinds) if k not in mid_first] + late
    started = []

    def source(k, s, far, own):
        if own and not far:
            return ins[k]
        return outs[k].at[index_of(s, (1 - m) if far else m, c)]

    def target(k, s, far):
        return outs[k].at[index_of(s, (1 - m) if far else m, c)]

    def line_copy(k, s, far, own, step):
        return remote(
            source(k, s, far, own),
            target(k, s, far),
            line_s.at[0 if step > 0 else 1, far, s, k],
            line_r.at[far, s, k],
            index_of(o + step, m, c),
        )

    def mid_copy(k, s, own):
        return remote(
            source(k, s, 0, own), target(k, s, 0), mid_s.at[s, k], mid_r.at[s, k], mid_peer
        )

    def core_copy(k, s, far, own):
        return remote(
            source(k, s, far, own),
            target(k, s, far),
            core_s.at[far, s, k],
            core_r.at[far, s, k],
            core_peer,
        )

    def begin(make, *conditions):
        def run():
            make().start()

        guarded(run, conditions)
        started.append((make, conditions))

    def guarded(run, conditions):
        if conditions:
            together = conditions[0]
            for other in conditions[1:]:
                together = jnp.logical_and(together, other)
            pl.when(together)(run)
        else:
            run()

    def spread(k, far):
        begin(lambda: line_copy(k, o, far, True, 1), o < outer - 1)
        begin(lambda: line_copy(k, o, far, True, -1), o > 0)

    for k in late:
        begin(lambda k=k: mid_copy(k, o, True))
    for k in order:
        spread(k, 0)
        if k not in mid_first:
            begin(lambda k=k: mid_copy(k, o, True))
        begin(lambda k=k: core_copy(k, o, 0, True))
        pltpu.make_async_copy(ins[k], target(k, o, 0), own_sem.at[k]).start()
    for k in late:
        mid_copy(k, o, True).wait_recv()
        spread(k, 1)
        begin(lambda k=k: core_copy(k, o, 1, True))
    for reach in range(1, outer):
        for k in order:
            for far in (0, 1) if k in mid_first else (0,):
                for side in (-1, 1):
                    s = o + side * reach
                    valid = s >= 0 if side < 0 else s < outer
                    more = o < outer - 1 if side < 0 else o > 0

                    def arrive(k=k, s=s, far=far, side=side):
                        line_copy(k, s, far, False, -side).wait_recv()

                    guarded(arrive, (valid,))
                    begin(
                        lambda k=k, s=s, far=far, side=side: line_copy(k, s, far, False, -side),
                        valid,
                        more,
                    )
                    if k not in mid_first:
                        begin(lambda k=k, s=s: mid_copy(k, s, False), valid)
                    begin(lambda k=k, s=s, far=far: core_copy(k, s, far, False), valid)
    for reach in range(outer):
        for k in order:
            if k in mid_first:
                continue
            for side in (-1, 1) if reach else (1,):
                s = o + side * reach
                limits = (s >= 0 if side < 0 else s < outer,) if reach else ()

                def arrive(k=k, s=s):
                    mid_copy(k, s, False).wait_recv()

                guarded(arrive, limits)
                begin(lambda k=k, s=s: core_copy(k, s, 1, False), *limits)
    for k in order:
        for s in range(outer):
            for far in range(2):
                core_copy(k, s, far, False).wait_recv()
    for make, conditions in started:
        guarded(lambda make=make: make().wait_send(), conditions)
    for k in order:
        pltpu.make_async_copy(ins[k], target(k, o, 0), own_sem.at[k]).wait()


def scatter_line_kernel(count, kinds, mid_last, *refs):
    ins, outs = refs[:kinds], refs[kinds : 2 * kinds]
    near, middle, last = (refs[(2 + i) * kinds : (3 + i) * kinds] for i in range(3))
    core_s, core_r, mid_s, mid_r, line_s, line_r = refs[5 * kinds :]
    o, m, c, outer = place_of(count)
    mid_peer, core_peer = index_of(o, 1 - m, c), index_of(o, m, 1 - c)
    greet(o, m, c, outer)
    early = [k for k in range(kinds) if k in mid_last]
    others = [k for k in range(kinds) if k not in mid_last]
    started = []

    def guarded(run, conditions):
        if conditions:
            together = conditions[0]
            for other in conditions[1:]:
                together = jnp.logical_and(together, other)
            pl.when(together)(run)
        else:
            run()

    def begin(make, *conditions):
        guarded(lambda: make().start(), conditions)
        started.append((make, conditions))

    def shard(s, far, core):
        return index_of(s, (1 - m) if far else m, core)

    def core_copy(k, s, far):
        return remote(
            ins[k].at[shard(s, far, 1 - c)],
            near[k].at[far, s],
            core_s.at[far, s, k],
            core_r.at[far, s, k],
            core_peer,
        )

    def mid_copy(k, s):
        return remote(
            near[k].at[1, s], middle[k].at[s], mid_s.at[s, k], mid_r.at[s, k], mid_peer
        )

    def line_copy(k, t, far, step, slot):
        return remote(
            near[k].at[far, t],
            last[k].at[far, slot],
            line_s.at[far, t, k],
            line_r.at[far, slot, k],
            index_of(o + step, m, c),
        )

    def targets(reach):
        if reach == 0:
            return [(o, 0, ())]
        return [(o + reach, 1, (o + reach < outer,)), (o - reach, -1, (o - reach >= 0,))]

    def pool(k, t, far):
        core_copy(k, t, far).wait_recv()
        near[k][far, t] = add(near[k][far, t], ins[k][shard(t, far, c)])

    def absorb(k, t, far, slot, step):
        line_copy(k, t, far, step, slot).wait_recv()
        near[k][far, t] = add(near[k][far, t], last[k][far, slot])

    far_to_near = list(range(outer - 1, -1, -1))
    for far in (1, 0):
        for reach in far_to_near:
            for k in others + early:
                for t, _, limits in targets(reach):
                    begin(lambda k=k, t=t, far=far: core_copy(k, t, far), *limits)
    for reach in far_to_near:
        for k in others:
            for t, _, limits in targets(reach):
                guarded(lambda k=k, t=t: pool(k, t, 1), limits)
                begin(lambda k=k, t=t: mid_copy(k, t), *limits)
    for reach in far_to_near:
        for k in early + others:
            for far in (1, 0) if k in mid_last else (0,):
                for t, step, limits in targets(reach):

                    def ready(k=k, t=t, far=far):
                        pool(k, t, far)
                        if k not in mid_last:
                            mid_copy(k, t).wait_recv()
                            near[k][0, t] = add(near[k][0, t], middle[k][t])

                    guarded(ready, limits)
                    from_left = lambda k=k, t=t, far=far: absorb(k, t, far, t, 1)
                    from_right = lambda k=k, t=t, far=far, slot=t: absorb(k, t, far, slot, -1)
                    if step >= 0:
                        guarded(from_left, limits + (o > 0,))
                    if step < 0:
                        guarded(from_right, limits + (o < outer - 1,))
                    if step == 0:
                        guarded(
                            lambda k=k, t=t, far=far: absorb(k, t, far, outer, -1),
                            (o < outer - 1,),
                        )
                        if far:
                            begin(lambda k=k, t=t: mid_copy(k, t))
                    else:
                        slot = outer if step < 0 and reach == 1 else t
                        begin(
                            lambda k=k, t=t, far=far, step=step, slot=slot: line_copy(
                                k, t, far, step, slot
                            ),
                            *limits,
                        )
    for k in others + early:
        total = near[k][0, o].astype(jnp.float32)
        if k in mid_last:
            mid_copy(k, o).wait_recv()
            total = total + middle[k][o].astype(jnp.float32)
        outs[k][...] = total
    for make, conditions in started:
        guarded(lambda make=make: make().wait_send(), conditions)


def gather_line(count, arrays, mid_first):
    kinds, outer = len(arrays), count // 4
    anywhere = pl.BlockSpec(memory_space=pl.ANY)
    dma = pltpu.SemaphoreType.DMA
    return pl.pallas_call(
        functools.partial(gather_line_kernel, count, kinds, mid_first),
        out_shape=[jax.ShapeDtypeStruct((count,) + a.shape, a.dtype) for a in arrays],
        in_specs=[anywhere] * kinds,
        out_specs=[anywhere] * kinds,
        scratch_shapes=[
            dma((kinds,)),
            dma((2, 2, outer, kinds)),
            dma((2, outer, kinds)),
            dma((outer, kinds)),
            dma((outer, kinds)),
            dma((2, outer, kinds)),
            dma((2, outer, kinds)),
        ],
        compiler_params=pltpu.CompilerParams(collective_id=2, has_side_effects=True),
        name="gather_line",
    )(*arrays)


def scatter_line(count, arrays, mid_last):
    kinds, outer = len(arrays), count // 4
    fast = pl.BlockSpec(memory_space=pltpu.VMEM)
    dma = pltpu.SemaphoreType.DMA
    return pl.pallas_call(
        functools.partial(scatter_line_kernel, count, kinds, mid_last),
        out_shape=[jax.ShapeDtypeStruct(a.shape[1:], jnp.float32) for a in arrays],
        in_specs=[fast] * kinds,
        out_specs=[fast] * kinds,
        scratch_shapes=[pltpu.VMEM((2, outer) + a.shape[1:], a.dtype) for a in arrays]
        + [pltpu.VMEM((outer,) + a.shape[1:], a.dtype) for a in arrays]
        + [
            pltpu.VMEM((2 if k in mid_last else 1, outer + 1) + a.shape[1:], a.dtype)
            for k, a in enumerate(arrays)
        ]
        + [
            dma((2, outer, kinds)),
            dma((2, outer, kinds)),
            dma((outer, kinds)),
            dma((outer, kinds)),
            dma((2, outer, kinds)),
            dma((2, outer + 1, kinds)),
        ],
        compiler_params=pltpu.CompilerParams(
            collective_id=3, has_side_effects=True, vmem_limit_bytes=56 * 2**20
        ),
        name="scatter_line",
    )(*arrays)


def gather_all(count, arrays):
    kinds, outer = len(arrays), count // 4
    if outer <= 4:
        return gather_line(count, arrays, (1,))
    anywhere = pl.BlockSpec(memory_space=pl.ANY)
    dma = pltpu.SemaphoreType.DMA
    return pl.pallas_call(
        functools.partial(gather_kernel, count, kinds),
        out_shape=[jax.ShapeDtypeStruct((count,) + a.shape, a.dtype) for a in arrays],
        in_specs=[anywhere] * kinds,
        out_specs=[anywhere] * kinds,
        scratch_shapes=[
            dma((kinds,)),
            dma((outer - 1, kinds)),
            dma((outer - 1, kinds)),
            dma((outer, kinds)),
            dma((outer, kinds)),
            dma((2, outer, kinds)),
            dma((2, outer, kinds)),
        ],
        compiler_params=pltpu.CompilerParams(collective_id=0, has_side_effects=True),
        name="gather_weights",
    )(*arrays)


def add(left, right):
    return (left.astype(jnp.float32) + right.astype(jnp.float32)).astype(left.dtype)


def scatter_kernel(count, kinds, *refs):
    ins, outs = refs[:kinds], refs[kinds : 2 * kinds]
    near, middle, last = (refs[(2 + i) * kinds : (3 + i) * kinds] for i in range(3))
    core_s, core_r, mid_s, mid_r, outer_s, outer_r = refs[5 * kinds :]
    o, m, c, outer = place_of(count)
    mid_peer, core_peer = index_of(o, 1 - m, c), index_of(o, m, 1 - c)
    greet(o, m, c, outer)
    order = list(range(1, outer)) + [0]
    started = []

    def begin(copy):
        copy.start()
        started.append(copy)

    def shard(r, far, core):
        return index_of(lax.rem(o + r, outer), (1 - m) if far else m, core)

    def core_copy(k, r, far):
        return remote(
            ins[k].at[shard(r, far, 1 - c)],
            near[k].at[far, r],
            core_s.at[far, r, k],
            core_r.at[far, r, k],
            core_peer,
        )

    def mid_copy(k, r):
        return remote(
            near[k].at[1, r], middle[k].at[r], mid_s.at[r, k], mid_r.at[r, k], mid_peer
        )

    def outer_copy(k, r):
        return remote(
            middle[k].at[r],
            last[k].at[r - 1],
            outer_s.at[r - 1, k],
            outer_r.at[r - 1, k],
            index_of(lax.rem(o + r, outer), m, c),
        )

    for far in (1, 0):
        for k in range(kinds):
            for r in order:
                begin(core_copy(k, r, far))
    for far in (1, 0):
        for k in range(kinds):
            for r in order:
                core_copy(k, r, far).wait_recv()
                near[k][far, r] = add(near[k][far, r], ins[k][shard(r, far, c)])
                if far:
                    begin(mid_copy(k, r))
    for k in range(kinds):
        for r in order:
            mid_copy(k, r).wait_recv()
            middle[k][r] = add(middle[k][r], near[k][0, r])
            if r:
                begin(outer_copy(k, r))
    for k in range(kinds):
        total = middle[k][0].astype(jnp.float32)
        for r in range(1, outer):
            outer_copy(k, r).wait_recv()
            total = total + last[k][r - 1].astype(jnp.float32)
        outs[k][...] = total
    for copy in started:
        copy.wait_send()


def scatter_all(count, arrays):
    kinds, outer = len(arrays), count // 4
    if outer <= 4:
        return scatter_line(count, arrays, (1,))
    fast = pl.BlockSpec(memory_space=pltpu.VMEM)
    dma = pltpu.SemaphoreType.DMA
    return pl.pallas_call(
        functools.partial(scatter_kernel, count, kinds),
        out_shape=[jax.ShapeDtypeStruct(a.shape[1:], jnp.float32) for a in arrays],
        in_specs=[fast] * kinds,
        out_specs=[fast] * kinds,
        scratch_shapes=[pltpu.VMEM((2, outer) + a.shape[1:], a.dtype) for a in arrays]
        + [pltpu.VMEM((outer,) + a.shape[1:], a.dtype) for a in arrays]
        + [pltpu.VMEM((outer - 1,) + a.shape[1:], a.dtype) for a in arrays]
        + [
            dma((2, outer, kinds)),
            dma((2, outer, kinds)),
            dma((outer, kinds)),
            dma((outer, kinds)),
            dma((outer - 1, kinds)),
            dma((outer - 1, kinds)),
        ],
        compiler_params=pltpu.CompilerParams(
            collective_id=1, has_side_effects=True, vmem_limit_bytes=56 * 2**20
        ),
        name="scatter_gradients",
    )(*arrays)


def dense_shape(rows, columns):
    if rows % 16 == 0:
        return (rows, columns)
    return (rows * columns // 128, 128)


def on_device(
    count,
    inputs,
    cotangent,
    segments,
    qkv_weight,
    out_weight,
    up_weight,
    down_weight,
    norm_params,
    bias_params,
    up_bias,
):
    is_first = lax.axis_index("section") == 0
    large = (qkv_weight[0], out_weight[0], up_weight[0], down_weight[0])
    shapes = [dense_shape(*piece.shape) for piece in large]
    narrow = norm_params.shape[2]
    fields = (4 * narrow, 4 * narrow, up_bias.shape[1])
    used = sum(fields)
    small = jnp.concatenate(
        [norm_params[0].reshape(-1), bias_params[0].reshape(-1), up_bias[0]]
    )
    padded = -(-used // 2048) * 2048
    small = jnp.pad(small, (0, padded - used)).reshape(-1, 128)
    gathered = gather_all(
        count, [small] + [piece.reshape(shape) for piece, shape in zip(large, shapes)]
    )
    flat = gathered[0].reshape(count, padded)
    norm_all = (
        flat[:, : fields[0]].reshape(count, 4, narrow).transpose(1, 0, 2).reshape(4, D)
    )
    bias_all = (
        flat[:, fields[0] : fields[0] + fields[1]]
        .reshape(count, 4, narrow)
        .transpose(1, 0, 2)
        .reshape(4, D)
    )
    up_bias_all = flat[:, fields[0] + fields[1] : used].reshape(FF)
    weights = tuple(
        whole.reshape(count * piece.shape[0], piece.shape[1])
        for whole, piece in zip(gathered[1:], large)
    ) + (norm_all, bias_all, up_bias_all)

    seg = segments.reshape(-1, PACK)
    tables = rotary_tables(seg)
    early, _ = forward(inputs, tables, weights)
    arrived = send_forward(early)
    layer_in = jnp.where(is_first, inputs, arrived)
    layer_out, saved_state = forward(layer_in, tables, weights)
    early_grad, _ = backward(saved_state, cotangent, tables, weights)
    returned = send_back(early_grad)
    upstream = jnp.where(is_first, returned, cotangent)
    input_grad, grads = backward(saved_state, upstream, tables, weights)

    small_grad = jnp.concatenate(
        [
            grads[4].reshape(4, count, narrow).transpose(1, 0, 2).reshape(count, -1),
            grads[5].reshape(4, count, narrow).transpose(1, 0, 2).reshape(count, -1),
            grads[6].reshape(count, -1),
        ],
        axis=1,
    )
    padded_grad = -(-used // 1024) * 1024
    small_grad = jnp.pad(small_grad, ((0, 0), (0, padded_grad - used)))
    owned = scatter_all(
        count,
        [small_grad.reshape(count, -1, 128)]
        + [
            grad.astype(jnp.bfloat16).reshape((count,) + shape)
            for grad, shape in zip(grads[:4], shapes)
        ],
    )
    tiny = owned[0].reshape(-1)
    result = [
        whole.reshape((1,) + piece.shape) for whole, piece in zip(owned[1:], large)
    ]
    return (
        layer_out[None],
        input_grad[None],
        *result,
        tiny[: fields[0]].reshape(1, 4, narrow),
        tiny[fields[0] : fields[0] + fields[1]].reshape(1, 4, narrow),
        tiny[fields[0] + fields[1] : used].reshape(1, -1),
    )


def solution(mesh):
    in_specs = (
        P("dp", None),
        P("dp", None),
        P("dp"),
        P("section", "dp", None),
        P("section", "dp", None),
        P("section", "dp", None),
        P("section", "dp", None),
        P("section", None, "dp"),
        P("section", None, "dp"),
        P("section", "dp"),
    )
    out_specs = (
        P("section", "dp", None),
        P("section", "dp", None),
        P("section", "dp", None),
        P("section", "dp", None),
        P("section", "dp", None),
        P("section", "dp", None),
        P("section", None, "dp"),
        P("section", None, "dp"),
        P("section", "dp"),
    )
    return jax.shard_map(
        functools.partial(on_device, mesh.shape["dp"]), mesh=mesh, in_specs=in_specs, out_specs=out_specs, check_vma=False
    )
```
